32 devices in a mesh: groups: 2 (over y), tm: 4 (over z), rows: 4 (over x, core).
Axes of the slice: x: 2, y: 2, z: 4, core: 2. Of those that a mesh axis runs over, the one named last changes fastest.
Arguments:
- inputs: bfloat16 [8, 16, 4, 19968], P('groups', 'tm', 'rows'), parts along dimension 0, may hold values from -6 to 6
- cotangent: bfloat16 [8, 16, 4, 19968], P('groups', 'tm', 'rows'), parts along dimension 0, may hold values from -6 to 6
- kernel: bfloat16 [27, 192, 192], replicated, may hold values from -0.078125 to 0.078125
- span_frames: int32 [8], P('groups'), parts along dimension 0, may hold values from 1 to 4, as said below
Outputs:
- grad_inputs: bfloat16 [8, 16, 4, 19968], P('groups', 'tm', 'rows'), parts along dimension 0
- weight_grad: float32 [54, 192, 192], P('groups', 'tm', 'rows'), parts along dimension 0
The draws below stay inside these ranges and needn't reach their ends.
There are 2 independent parts, one for each index of `groups`. The reference program is written for one: setup_inputs(seed, part) draws one part's arguments, and reference() takes and returns one part's arrays. A program takes and returns all parts, laid end to end along the dimension named above; an argument that names none is the same for every part. Nothing has to cross between parts.
Inputs may be any that keep to these rules, and one draw needn't show every extreme that they name: Entry 0 is 1. Time span c holds span_frames[c] consecutive frames of every video in its first slots, the frames following those of span c - 1; its other slots hold no frame, and inputs and cotangent there are not read.
All inputs are finite; a program needn't handle non-finite values.
Results may differ from the reference program's by a relative error of at most 0.0031.
Values may be sent and summed in bfloat16 or wider, within the bound.
A program may use at most 192 MiB of HBM per device.

```python
import jax
import jax.numpy as jnp
from jax import lax

CH = 192
TAPS = 27
GRID_W = 104
BATCH = 4
SLOTS_DEV = 4
SPANS = 4
SLOTS = 16
HEIGHT = 4
CELLS = 26624


def draw_span_frames(key, part):
    key_counts = jax.random.fold_in(key, 101)
    key_order = jax.random.fold_in(key, 202)
    counts = jax.random.randint(key_counts, (SPANS,), 1, SLOTS_DEV + 1).astype(jnp.int32)
    shuffled = jax.random.permutation(key_order, SPANS - 1).astype(jnp.int32) + 1
    chosen = shuffled[0]
    order = jnp.arange(SPANS, dtype=jnp.int32)
    counts = jnp.where(order == chosen, SLOTS_DEV, counts)
    counts = jnp.where(order == 0, 1, counts)
    return counts.astype(jnp.int32)


def level_of(own_key, shape, cuts, least, high):
    def one(position, blocks):
        heights = jax.random.uniform(jax.random.fold_in(jax.random.fold_in(own_key, 6), position), (blocks,), jnp.float32, least / len(cuts), high / len(cuts))
        return jnp.repeat(jnp.exp(heights), shape[position] // blocks).reshape((-1,) + (1,) * (len(shape) - position - 1))

    factor_of = one(*cuts[0])
    for cut in cuts[1:]:
        factor_of = factor_of * one(*cut)
    return factor_of


def bell_draw(rng, dims, width, most, shards=(), kind=jnp.bfloat16):
    entries = width * jax.random.normal(rng, dims, jnp.float32)
    if shards:
        entries = entries * level_of(rng, dims, shards, -0.22, 0.18)
    return jnp.clip(entries, -most, most).astype(kind)


def setup_inputs(seed: int = 0, part: int = 0) -> dict:
    key_list = jax.random.split(jax.random.key(seed), 5)
    part_keys = jax.random.split(jax.random.fold_in(key_list[4], part), 5)
    inputs = bell_draw(part_keys[0], (BATCH, SLOTS, HEIGHT, GRID_W * CH), 1.0, 6.0, ((1, 4), (2, 4)))
    cotangent = bell_draw(part_keys[1], (BATCH, SLOTS, HEIGHT, GRID_W * CH), 1.0, 6.0, ((1, 4), (2, 4)))
    kernel = bell_draw(key_list[2], (TAPS, CH, CH), (TAPS * CH) ** -0.5, 0.078125)
    span_frames = draw_span_frames(jax.random.fold_in(jax.random.fold_in(key_list[4], part), 71), part)
    return {"inputs": inputs, "cotangent": cotangent, "kernel": kernel, "span_frames": span_frames}


def reference(inputs, cotangent, kernel, span_frames):
    batch, slots, height, flat = inputs.shape
    per_span = slots // SPANS
    starts = (jnp.cumsum(span_frames) - span_frames).astype(jnp.int32)
    slot_ids = jnp.arange(slots, dtype=jnp.int32)
    span_ids = (slot_ids // per_span).astype(jnp.int32)
    within = (slot_ids % per_span).astype(jnp.int32)
    live = within < span_frames[span_ids]
    target = jnp.where(live, starts[span_ids] + within, slots).astype(jnp.int32)
    values = inputs.astype(jnp.float32)
    sigma = jax.nn.sigmoid(values)
    silu_out = (values * sigma).astype(jnp.bfloat16)
    compact_act = jnp.zeros_like(silu_out).at[:, target].set(silu_out, mode="drop")
    compact_grad = jnp.zeros_like(cotangent).at[:, target].set(cotangent, mode="drop")
    act_pad = jnp.pad(compact_act.reshape(batch, slots, height, GRID_W, CH), ((0, 0), (2, 0), (1, 1), (1, 1), (0, 0)))
    grad_pad = jnp.pad(compact_grad.reshape(batch, slots, height, GRID_W, CH), ((0, 0), (0, 2), (1, 1), (1, 1), (0, 0)))
    grad_flat = compact_grad.reshape(-1, CH)
    cell_count = grad_flat.shape[0]
    adjoint = jnp.zeros((cell_count, CH), jnp.float32)
    pieces = []
    for frame_off in range(3):
        for row_off in range(3):
            for col_off in range(3):
                tap_index = 9 * frame_off + 3 * row_off + col_off
                window = act_pad[:, frame_off:frame_off + slots, row_off:row_off + height, col_off:col_off + GRID_W].reshape(cell_count, CH)
                pieces.append(lax.dot_general(window, grad_flat, (((0,), (0,)), ((), ())), preferred_element_type=jnp.float32))
                mirror = grad_pad[:, 2 - frame_off:2 - frame_off + slots, 2 - row_off:2 - row_off + height, 2 - col_off:2 - col_off + GRID_W].reshape(cell_count, CH)
                adjoint = adjoint + lax.dot_general(mirror, kernel[tap_index], (((1,), (1,)), ((), ())), preferred_element_type=jnp.float32)
    adjoint = adjoint.reshape(batch, slots, height, flat)
    gathered = adjoint[:, jnp.minimum(target, slots - 1)]
    slope = sigma * (1.0 + values * (1.0 - sigma))
    mask = live[None, :, None, None]
    grad_inputs = jnp.where(mask, gathered * slope, jnp.zeros_like(slope)).astype(jnp.bfloat16)
    weight_grad = jnp.stack(pieces) * (CELLS ** -0.5)
    return grad_inputs, weight_grad
```

```python
import functools

import jax
import jax.numpy as jnp
from jax import lax
from jax.experimental import pallas as pl
from jax.experimental.pallas import tpu as pltpu
from jax.sharding import PartitionSpec as P

CH = 192
PAIR = 2 * CH
LANES = 128
MESH = pl.DeviceIdType.MESH
F32, BF16 = jnp.float32, jnp.bfloat16

OWN, CORE, FAR = 0, 1, 2
BLOCKS = ((OWN, 0), (CORE, 0), (OWN, 1), (CORE, 1), (OWN, 2), (CORE, 2), (FAR, 1), (FAR, 2), (FAR, 0))
WIDE = len(BLOCKS) * CH
COL = {block: CH * n for n, block in enumerate(BLOCKS)}
PARTS = (((OWN, 0), (OWN, 1)), ((CORE, 0), (FAR, 0)), ((CORE, 1), (FAR, 1)), ((CORE, 2), (FAR, 2)), ((OWN, 2),))
SPOT = {block: (m, n) for m, part in enumerate(PARTS) for n, block in enumerate(part)}


def matmul(a, b):
    return lax.dot_general(a, b, (((1,), (0,)), ((), ())), preferred_element_type=F32)


def kernel_body(cells, batch, slots, strips, spans, factor, frames_ref, x_hbm, cot_hbm, kern_hbm, out_ref, share_ref,
                xv, cv, tmp, own, near, far_in, far, act, act_t, slope, wide_g, kern, kern_t,
                t_send, t_recv, t_core, t_far, wgs, got1, send2, got2, zfull, zsend, got3,
                s_in, s_near, r_near, s_t, r_t, s_tc, r_tc, s_tf, r_tf, s1, r1, s2, r2, s3, r3):
    frames = batch * slots
    pairs = cells // 2
    tiles = PAIR // LANES
    wide, part, half = CH // strips, CH // spans, strips // 2
    row = lax.axis_index("rows")
    span = lax.axis_index("tm")
    place = row // 2
    parity = row - 2 * place
    other = 1 - parity
    partner = 2 * place + other
    beside = row + 2 * parity - 1
    has_far = (beside >= 0) & (beside < strips)
    far_row = lax.rem(beside + strips, strips)
    first, last = span == 0, span == spans - 1
    before = lax.rem(span + spans - 1, spans)

    def strip_at(d):
        return lax.rem(place + d, half)

    def remote(src, dst, send, recv, **to):
        return pltpu.make_async_remote_copy(src, dst, send, recv, device_id=to, device_id_type=MESH)

    get_cot = pltpu.make_async_copy(cot_hbm, cv, s_in.at[0])
    get_x = pltpu.make_async_copy(x_hbm, xv, s_in.at[1])
    get_kern = pltpu.make_async_copy(kern_hbm, kern, s_in.at[2])
    get_cot.start()
    get_x.start()
    get_kern.start()
    barrier = pltpu.get_barrier_semaphore()
    for d in range(1, strips):
        pl.semaphore_signal(barrier, inc=1, device_id={"rows": lax.rem(row + d, strips)}, device_id_type=MESH)
    for d in range(1, spans):
        pl.semaphore_signal(barrier, inc=1, device_id={"tm": lax.rem(span + d, spans)}, device_id_type=MESH)

    core_copy = remote(own, near, s_near.at[0], r_near.at[0], rows=partner)
    far_copy = remote(cot_hbm, far_in, s_near.at[1], r_near.at[1], rows=far_row)
    tail_copies = [remote(t_send.at[n], t_recv.at[n], s_t.at[n], r_t.at[n], tm=before) for n in range(2)]
    tail_core = [remote(t_recv.at[n], t_core.at[n], s_tc.at[n], r_tc.at[n], rows=partner) for n in range(2)]
    tail_far = [remote(t_recv.at[n], t_far.at[n], s_tf.at[n], r_tf.at[n], rows=far_row) for n in range(2)]

    pl.semaphore_wait(barrier, strips + spans - 2)
    pl.when(has_far)(far_copy.start)

    count = frames_ref[span]
    slot_of = lax.broadcasted_iota(jnp.int32, (frames, PAIR), 0) // batch

    def flag(condition):
        return jnp.where(condition, 1.0, 0.0).astype(BF16)

    def by_slot(ref, p):
        base = tiles * lax.rem(p, 2)
        at = pl.multiple_of(p * PAIR, LANES)
        for b in range(batch):
            v = ref[b, :, pl.ds(at, PAIR)].astype(F32)
            for t in range(tiles):
                tmp[base + t, pl.ds(b, slots, stride=batch), :] = v[:, LANES * t:LANES * (t + 1)]
        return jnp.concatenate([tmp[base + t] for t in range(tiles)], axis=1)

    def put(v, p, col):
        wide_g[2 * p + 1, :, col:col + CH] = v[:, :CH]
        wide_g[2 * p + 2, :, col:col + CH] = v[:, CH:]

    def arrange(ref, dst, col):
        def one(p, carry):
            v = by_slot(ref, p).astype(BF16)
            dst[p] = v
            put(v, p, col)
            return carry

        lax.fori_loop(0, pairs, one, 0, unroll=2)

    def plain(src, col):
        def one(p, carry):
            put(src[p], p, col)
            return carry

        lax.fori_loop(0, pairs, one, 0, unroll=4)

    def spread(tail, q):
        rows = tail[q * batch:(q + 1) * batch]
        return jnp.concatenate([rows] * slots, axis=0)

    def later(src, tails, d, col):
        keep = flag(slot_of + d < count)
        at_one = flag(slot_of + d == count)
        at_two = flag(slot_of + d > count)

        def one(g, carry):
            one_rows = tails[0, g]
            two_rows = tails[1, g] if d == 2 else None
            for q in range(slots):
                p = slots * g + q
                v = src[p]
                v = jnp.concatenate([v[d * batch:], v[:d * batch]], axis=0) * keep
                if d == 1:
                    v = v + spread(one_rows, q) * (1.0 - keep).astype(BF16)
                else:
                    v = v + spread(one_rows, q) * at_one + spread(two_rows, q) * at_two
                put(v, p, col)
            return carry

        lax.fori_loop(0, pairs // slots, one, 0)

    zero = jnp.zeros((frames, WIDE), BF16)
    wide_g[0] = zero
    wide_g[cells + 1] = zero

    @pl.when(last)
    def _():
        t_recv[...] = jnp.zeros(t_recv.shape, BF16)

    @pl.when(jnp.logical_not(has_far))
    def _():
        far_in[...] = jnp.zeros(far_in.shape, BF16)
        t_far[...] = jnp.zeros(t_far.shape, BF16)

    get_cot.wait()
    arrange(cv, own, COL[OWN, 0])
    core_copy.start()

    def pack_first(g, carry):
        t_send[0, g] = jnp.concatenate([own[slots * g + q][:batch] for q in range(slots)], axis=0)
        return carry

    lax.fori_loop(0, pairs // slots, pack_first, 0)
    pl.when(jnp.logical_not(first))(tail_copies[0].start)

    get_x.wait()
    live = (slot_of < count)[:, :CH]

    def activate(p, carry):
        v = by_slot(xv, p)
        for q in range(2):
            xf = v[:, q * CH:(q + 1) * CH]
            s = 1.0 / (1.0 + jnp.exp(-xf))
            act[2 * p + q] = jnp.where(live, xf * s, 0.0).astype(BF16)
            slope[2 * p + q] = jnp.where(live, s * (1.0 + xf * (1.0 - s)), 0.0)
        return carry

    lax.fori_loop(0, pairs, activate, 0, unroll=2)

    group = LANES // frames

    def turn(k, carry):
        v = act[pl.ds(k * group, group)].reshape(LANES, CH)
        act_t[:, pl.ds(pl.multiple_of(k * LANES, LANES), LANES)] = v.T
        return carry

    lax.fori_loop(0, cells // group, turn, 0)

    core_copy.wait_recv()
    plain(near, COL[CORE, 0])

    def weight(blocks):
        lo, n = COL[blocks[0]], CH * len(blocks)
        for c in range(3):
            g = wide_g[pl.ds(2 - c, cells), :, lo:lo + n].reshape(cells * frames, n)
            turned = matmul(act_t[...], g).T
            for k, block in enumerate(blocks):
                m, spot = SPOT[block]
                at = CH * (3 * spot + c)
                for s in range(strips):
                    lo_row = CH * k + wide * s
                    wgs[m][s, :, at:at + CH] = turned[lo_row:lo_row + wide]

    order = list(range(1, half)) + [0]
    copies1, copies2, copies3 = {}, {}, {}

    def start_core(m):
        copies1[m] = []
        for d in order:
            cp = remote(wgs[m].at[2 * strip_at(d) + other], got1[m].at[d], s1.at[m, d], r1.at[m, d], rows=partner)
            cp.start()
            copies1[m].append(cp)

    def chip_sum(m, to, d):
        theirs = got1[m][d]
        if PARTS[m][0][0] == CORE:
            theirs = jnp.concatenate([theirs[:, 3 * CH:], theirs[:, :3 * CH]], axis=1)
        return wgs[m][to] + theirs

    def start_rows(m):
        copies2[m] = []
        for d, cp in zip(order, copies1[m]):
            cp.wait()
            if d:
                to = 2 * strip_at(d) + parity
                send2[m][d - 1] = chip_sum(m, to, d).astype(BF16)
                nxt = remote(send2[m].at[d - 1], got2[m].at[d - 1], s2.at[m, d - 1], r2.at[m, d - 1], rows=to)
                nxt.start()
                copies2[m].append(nxt)

    thick = 16 if wide % 16 == 0 else wide

    def start_spans(m):
        total = chip_sum(m, row, 0)
        for d, cp in enumerate(copies2[m]):
            cp.wait()
            total = total + got2[m][d].astype(F32)
        taps = 3 * len(PARTS[m])
        for t in range(spans):
            pieces = [
                total[k:k + thick, CH * j + part * t:CH * j + part * (t + 1)]
                for k in range(0, wide, thick) for j in range(taps)
            ]
            piece = jnp.concatenate(pieces, axis=1)
            zfull[m][t] = piece
            zsend[m][t] = piece.astype(BF16)
        copies3[m] = []
        for d in range(1, spans):
            to = lax.rem(span + d, spans)
            cp = remote(zsend[m].at[to], got3[m].at[d - 1], s3.at[m, d - 1], r3.at[m, d - 1], tm=to)
            cp.start()
            copies3[m].append(cp)

    def tap_row(role):
        return {OWN: 1, CORE: 2 * parity, FAR: 2 - 2 * parity}[role]

    def finish(m):
        final = zfull[m][span]
        for d, cp in enumerate(copies3[m]):
            cp.wait()
            final = final + got3[m][d].astype(F32)
        taps = 3 * len(PARTS[m])
        n = taps * part
        final = jnp.concatenate([final[:, k * n:(k + 1) * n] for k in range(wide // thick)], axis=0) * factor
        final = final.T
        for spot, (role, d) in enumerate(PARTS[m]):
            for c in range(3):
                j = 3 * spot + c
                share_ref[9 * (2 - d) + 3 * tap_row(role) + c] = final[part * j:part * (j + 1)]

    step = 26 if cells % 26 == 0 else 2
    steps = cells // step

    def adjoint(j, carry):
        w0 = j * step
        acc = jnp.zeros((step * frames, CH), F32)
        for c in range(3):
            g = wide_g[pl.ds(w0 + 2 - c, step)].reshape(step * frames, WIDE)
            acc = acc + matmul(g, kern_t[c])
        res = acc.reshape(step, frames, CH) * slope[pl.ds(w0, step)]
        for p in range(step // 2):
            at = pl.multiple_of((w0 + 2 * p) * CH, LANES)
            v = jnp.concatenate([res[2 * p], res[2 * p + 1]], axis=1)
            base = tiles * (p % 2)
            for t in range(tiles):
                tmp[base + t] = v[:, LANES * t:LANES * (t + 1)]
            for t in range(tiles):
                for b in range(batch):
                    out_ref[b, :, pl.ds(at + LANES * t, LANES)] = tmp[base + t, pl.ds(b, slots, stride=batch), :].astype(BF16)
        return carry

    def turn_kern(c, carry):
        for n, (role, d) in enumerate(BLOCKS):
            kern_t[c, CH * n:CH * (n + 1), :] = kern[9 * (2 - d) + 3 * tap_row(role) + c].T
        return carry

    weight(((OWN, 0), (CORE, 0)))
    get_kern.wait()
    lax.fori_loop(0, 3, turn_kern, 0)

    pl.when(jnp.logical_not(last))(tail_copies[0].wait_recv)
    tail_core[0].start()
    pl.when(has_far)(tail_far[0].start)
    two = jnp.full((frames, PAIR), jnp.where(count >= 2, 1.0, 0.0), F32).astype(BF16)
    not_two = (1.0 - two).astype(BF16)

    def pack_second(g, carry):
        mine = jnp.concatenate([own[slots * g + q][batch:2 * batch] for q in range(slots)], axis=0)
        t_send[1, g] = mine * two + t_recv[0, g] * not_two
        return carry

    lax.fori_loop(0, pairs // slots, pack_second, 0)
    pl.when(jnp.logical_not(first))(tail_copies[1].start)
    later(own, t_recv, 1, COL[OWN, 1])
    tail_core[0].wait_recv()
    later(near, t_core, 1, COL[CORE, 1])
    weight(((OWN, 1), (CORE, 1)))
    start_core(0)

    pl.when(has_far)(far_copy.wait_recv)
    arrange(far_in, far, COL[FAR, 0])
    weight(((FAR, 0),))
    start_core(1)
    start_rows(0)

    pl.when(jnp.logical_not(last))(tail_copies[1].wait_recv)
    tail_core[1].start()
    pl.when(has_far)(tail_far[1].start)
    later(own, t_recv, 2, COL[OWN, 2])
    tail_core[1].wait_recv()
    later(near, t_core, 2, COL[CORE, 2])
    weight(((OWN, 2), (CORE, 2)))
    start_core(4)
    start_rows(1)

    pl.when(has_far)(tail_far[0].wait_recv)
    later(far, t_far, 1, COL[FAR, 1])
    pl.when(has_far)(tail_far[1].wait_recv)
    later(far, t_far, 2, COL[FAR, 2])
    weight(((FAR, 1), (FAR, 2)))
    start_core(2)
    start_core(3)
    start_rows(4)

    lax.fori_loop(0, steps // 4, adjoint, 0)
    start_rows(2)
    start_rows(3)
    start_spans(0)
    lax.fori_loop(steps // 4, steps // 2, adjoint, 0)
    start_spans(1)
    start_spans(4)
    lax.fori_loop(steps // 2, 3 * steps // 4, adjoint, 0)
    start_spans(2)
    lax.fori_loop(3 * steps // 4, steps, adjoint, 0)
    start_spans(3)
    for m in (0, 1, 4, 2, 3):
        finish(m)

    core_copy.wait_send()
    pl.when(has_far)(far_copy.wait_send)
    for n in range(2):
        pl.when(jnp.logical_not(first))(tail_copies[n].wait_send)
        tail_core[n].wait_send()
        pl.when(has_far)(tail_far[n].wait_send)


def body(inputs, cotangent, kernel, span_frames):
    batch, slots, strip, flat = inputs.shape
    cells = flat // CH
    frames = batch * slots
    pairs = cells // 2
    spans, strips = lax.axis_size("tm"), lax.axis_size("rows")
    assert strip == 1 and batch == slots and frames == 16 and cells % 8 == 0
    assert strips % 2 == 0 and CH % spans == 0 and CH % strips == 0
    wide, part, half = CH // strips, CH // spans, strips // 2
    total_cells = batch * slots * spans * strip * strips * cells
    few, some = max(half - 1, 1), max(spans - 1, 1)
    thick = 16 if wide % 16 == 0 else wide
    widths = [3 * CH * len(p) for p in PARTS]
    zblocks = [(thick, wide // thick * 3 * len(p) * part) for p in PARTS]
    dma = pltpu.SemaphoreType.DMA
    parts = len(PARTS)

    def each(lead, shapes, kind):
        return tuple(pltpu.VMEM((lead,) + tuple(s), kind) for s in shapes)

    rows_of = [(wide, w) for w in widths]
    natural = (batch, slots, flat)
    paired = (pairs, frames, PAIR)
    tail = (2, pairs // slots, frames, PAIR)
    anywhere = pl.BlockSpec(memory_space=pl.ANY)
    vmem = pl.BlockSpec(memory_space=pltpu.VMEM)
    grad_in, share = pl.pallas_call(
        functools.partial(kernel_body, cells, batch, slots, strips, spans, float(total_cells) ** -0.5),
        out_shape=(
            jax.ShapeDtypeStruct(natural, BF16),
            jax.ShapeDtypeStruct((27, part, wide), F32),
        ),
        in_specs=[pl.BlockSpec(memory_space=pltpu.SMEM), anywhere, anywhere, anywhere],
        out_specs=(vmem, vmem),
        scratch_shapes=[
            pltpu.VMEM(natural, BF16),
            pltpu.VMEM(natural, BF16),
            pltpu.VMEM((2 * PAIR // LANES, frames, LANES), F32),
            pltpu.VMEM(paired, BF16),
            pltpu.VMEM(paired, BF16),
            pltpu.VMEM(natural, BF16),
            pltpu.VMEM(paired, BF16),
            pltpu.VMEM((cells, frames, CH), BF16),
            pltpu.VMEM((CH, cells * frames), BF16),
            pltpu.VMEM((cells, frames, CH), F32),
            pltpu.VMEM((cells + 2, frames, WIDE), BF16),
            pltpu.VMEM(kernel.shape, BF16),
            pltpu.VMEM((3, WIDE, CH), BF16),
            pltpu.VMEM(tail, BF16),
            pltpu.VMEM(tail, BF16),
            pltpu.VMEM(tail, BF16),
            pltpu.VMEM(tail, BF16),
            each(strips, rows_of, F32),
            each(half, rows_of, F32),
            each(few, rows_of, BF16),
            each(few, rows_of, BF16),
            each(spans, zblocks, F32),
            each(spans, zblocks, BF16),
            each(some, zblocks, BF16),
            dma((3,)), dma((2,)), dma((2,)), dma((2,)), dma((2,)), dma((2,)), dma((2,)), dma((2,)), dma((2,)),
            dma((parts, half)), dma((parts, half)), dma((parts, few)), dma((parts, few)),
            dma((parts, some)), dma((parts, some)),
        ],
        compiler_params=pltpu.CompilerParams(
            vmem_limit_bytes=56 << 20, collective_id=0, has_side_effects=True
        ),
        name="fused",
    )(span_frames, inputs.reshape(natural), cotangent.reshape(natural), kernel)
    return grad_in.reshape(inputs.shape), share


def solution(mesh):
    return jax.shard_map(
        body,
        mesh=mesh,
        in_specs=(
            P("groups", "tm", "rows", None),
            P("groups", "tm", "rows", None),
            P(),
            P("groups"),
        ),
        out_specs=(P("groups", "tm", "rows", None), P("groups", "tm", "rows")),
        check_vma=False,
    )
```

```python
import functools

import jax
import jax.numpy as jnp
from jax import lax
from jax.experimental import pallas as pl
from jax.experimental.pallas import tpu as pltpu
from jax.sharding import PartitionSpec as P

CH = 192
PAIR = 2 * CH
LANES = 128
MESH = pl.DeviceIdType.MESH
F32, BF16 = jnp.float32, jnp.bfloat16

OWN, CORE, FAR = 0, 1, 2
WIDE = 640
PARTS = (((OWN, 0), (OWN, 1)), ((CORE, 0), (FAR, 0)), ((CORE, 1), (FAR, 1)), ((CORE, 2), (FAR, 2)), ((OWN, 2),))
SPOT = {block: (m, n) for m, part in enumerate(PARTS) for n, block in enumerate(part)}


def down(v, n):
    return jnp.concatenate([jnp.zeros((n,) + v.shape[1:], v.dtype), v[:-n]], axis=0)


def up(v, n):
    return jnp.concatenate([v[n:], jnp.zeros((n,) + v.shape[1:], v.dtype)], axis=0)


def kernel_body(cells, batch, slots, strips, spans, factor, frames_ref, x_hbm, cot_hbm, kern_hbm, out_hbm, share_hbm,
                out_ref, share_ref, xv, cv, core_in, far_in, tmp, act, slope, wide_g, acc, kern, kern_n,
                second, t_send, t_recv, t_core, t_far, wgs, got1, send2, got2, zfull, zsend, got3,
                s_in, s_out, s_near, r_near, s_t, r_t, s_tc, r_tc, s_tf, r_tf, s1, r1, s2, r2, s3, r3):
    rows = 16
    quarters = rows // batch
    groups = cells // quarters
    pairs = groups // 2
    tiles = PAIR // LANES
    wide, part, half = CH // strips, CH // spans, strips // 2
    row = lax.axis_index("rows")
    span = lax.axis_index("tm")
    place = row // 2
    parity = row - 2 * place
    other = 1 - parity
    partner = 2 * place + other
    beside = row + 2 * parity - 1
    has_far = (beside >= 0) & (beside < strips)
    far_row = lax.rem(beside + strips, strips)
    first, last = span == 0, span == spans - 1
    before = lax.rem(span + spans - 1, spans)

    def strip_at(d):
        return lax.rem(place + d, half)

    def remote(src, dst, send, recv, **to):
        return pltpu.make_async_remote_copy(src, dst, send, recv, device_id=to, device_id_type=MESH)

    get_cot = pltpu.make_async_copy(cot_hbm, cv, s_in.at[0])
    get_x = pltpu.make_async_copy(x_hbm, xv, s_in.at[1])
    get_kern = pltpu.make_async_copy(kern_hbm, kern, s_in.at[2])
    get_cot.start()
    get_x.start()
    barrier = pltpu.get_barrier_semaphore()
    for d in range(1, strips):
        pl.semaphore_signal(barrier, inc=1, device_id={"rows": lax.rem(row + d, strips)}, device_id_type=MESH)
    for d in range(1, spans):
        pl.semaphore_signal(barrier, inc=1, device_id={"tm": lax.rem(span + d, spans)}, device_id_type=MESH)

    core_copy = remote(cot_hbm, core_in, s_near.at[0], r_near.at[0], rows=partner)
    far_copy = remote(cot_hbm, far_in, s_near.at[1], r_near.at[1], rows=far_row)
    tail_copies = [remote(t_send.at[n], t_recv.at[n], s_t.at[n], r_t.at[n], tm=before) for n in range(2)]
    tail_core = [remote(t_recv.at[n], t_core.at[n], s_tc.at[n], r_tc.at[n], rows=partner) for n in range(2)]
    tail_far = [remote(t_recv.at[n], t_far.at[n], s_tf.at[n], r_tf.at[n], rows=far_row) for n in range(2)]

    pl.semaphore_wait(barrier, strips + spans - 2)
    pl.when(has_far)(far_copy.start)
    core_copy.start()

    count = frames_ref[span]

    def where(condition):
        return jnp.where(condition, 1.0, 0.0)

    def load_pair(ref, p):
        base = tiles * p
        for k in range(quarters):
            at = k * groups * CH + p * PAIR
            for b in range(batch):
                v = ref[b, :, pl.ds(at, PAIR)].astype(F32)
                for t in range(tiles):
                    tmp[base + t, pl.ds(batch * k + b, slots, stride=rows), :] = v[:, LANES * t:LANES * (t + 1)]
        return [
            jnp.concatenate([tmp[base + t, rows * s:rows * (s + 1)] for t in range(tiles)], axis=1) for s in range(slots)
        ]

    def put(v, f, p, role):
        col = CH * role
        wide_g[f, 2 * p + 1, :, col:col + CH] = v[:, :CH]
        wide_g[f, 2 * p + 2, :, col:col + CH] = v[:, CH:]

    def edges(frames, role):
        lanes = pl.ds(CH * role, CH)
        for f in frames:
            wide_g[f, 0, :, lanes] = down(wide_g[f, groups, :, lanes], batch)
            wide_g[f, groups + 1, :, lanes] = up(wide_g[f, 1, :, lanes], batch)

    def arrange(ref, role):
        def one(p):
            for s, v in enumerate(load_pair(ref, p)):
                v = (v * where(s < count) if s else v).astype(BF16)
                put(v, s, p, role)
                if role == OWN and s == 0:
                    t_send[0, p] = v
                if role == OWN and s == 1:
                    second[p] = v

        for p in range(pairs):
            one(p)
        edges(range(slots), role)

    def extend(tails, n, role):
        for p in range(pairs):
            put(tails[n, p], slots + n, p, role)
        edges([slots + n], role)

    def blank(g, carry):
        for f in range(slots + 2):
            wide_g[f, g, :, 3 * CH:] = jnp.zeros((rows, WIDE - 3 * CH), BF16)
        return carry

    lax.fori_loop(0, groups + 2, blank, 0, unroll=4)

    @pl.when(last)
    def _():
        t_recv[...] = jnp.zeros(t_recv.shape, BF16)

    @pl.when(jnp.logical_not(has_far))
    def _():
        far_in[...] = jnp.zeros(far_in.shape, BF16)
        t_far[...] = jnp.zeros(t_far.shape, BF16)

    get_cot.wait()
    get_kern.start()
    arrange(cv, OWN)
    pl.when(jnp.logical_not(first))(tail_copies[0].start)

    def put_act(v, f, p):
        for q in range(2):
            cell = v[:, CH * q:CH * (q + 1)]
            for c in range(3):
                act[f, 2 * p + q + 2 - c, :, CH * c:CH * (c + 1)] = cell

    def activate(p):
        at_end, ahead = [jnp.zeros((rows, PAIR), F32)] * 2
        for s, xf in enumerate(load_pair(xv, p)):
            on = where(s < count)
            sig = 1.0 / (1.0 + jnp.exp(-xf))
            a = xf * sig * on
            put_act(a.astype(BF16), s, p)
            at_end = at_end + a * where(s == count - 1)
            ahead = ahead + a * where(s == count - 2)
            v = sig * (1.0 + xf * (1.0 - sig)) * on
            for q in range(2):
                slope[s, 2 * p + q] = v[:, CH * q:CH * (q + 1)]
        put_act(ahead.astype(BF16), slots, p)
        put_act(at_end.astype(BF16), slots + 1, p)

    get_x.wait()
    for p in range(pairs):
        activate(p)
    for f in range(slots + 2):
        act[f, 1, :, :CH] = down(act[f, groups + 1, :, :CH], batch)
        act[f, groups, :, 2 * CH:] = up(act[f, 0, :, 2 * CH:], batch)

    core_copy.wait_recv()
    arrange(core_in, CORE)

    def weight(roles, d):
        lo, n = CH * roles[0], CH * len(roles)
        m_rows = slots * groups * rows
        g = wide_g[d:d + slots, 1:groups + 1, :, lo:lo + n].reshape(m_rows, n)
        a = act[:slots - d, 1:groups + 1]
        if d:
            a = jnp.concatenate([a, act[slots + 2 - d:, 1:groups + 1]], axis=0)
        res = lax.dot_general(
            g, a.reshape(m_rows, 3 * CH), (((0,), (0,)), ((), ())), preferred_element_type=F32
        )
        for k, role in enumerate(roles):
            m, spot = SPOT[role, d]
            for s in range(strips):
                lo_row = CH * k + wide * s
                wgs[m][s, :, 3 * CH * spot:3 * CH * (spot + 1)] = res[lo_row:lo_row + wide]

    order = list(range(1, half)) + [0]
    copies1, copies2, copies3 = {}, {}, {}

    def start_core(m):
        copies1[m] = []
        for d in order:
            cp = remote(wgs[m].at[2 * strip_at(d) + other], got1[m].at[d], s1.at[m, d], r1.at[m, d], rows=partner)
            cp.start()
            copies1[m].append(cp)

    def chip_sum(m, to, d):
        theirs = got1[m][d]
        if PARTS[m][0][0] == CORE:
            theirs = jnp.concatenate([theirs[:, 3 * CH:], theirs[:, :3 * CH]], axis=1)
        return wgs[m][to] + theirs

    def start_rows(m):
        copies2[m] = []
        for d, cp in zip(order, copies1[m]):
            cp.wait()
            if d:
                to = 2 * strip_at(d) + parity
                send2[m][d - 1] = chip_sum(m, to, d).astype(BF16)
                nxt = remote(send2[m].at[d - 1], got2[m].at[d - 1], s2.at[m, d - 1], r2.at[m, d - 1], rows=to)
                nxt.start()
                copies2[m].append(nxt)

    thick = 16 if wide % 16 == 0 else wide

    def start_spans(m):
        total = chip_sum(m, row, 0)
        for d, cp in enumerate(copies2[m]):
            cp.wait()
            total = total + got2[m][d].astype(F32)
        taps = 3 * len(PARTS[m])
        for t in range(spans):
            pieces = [
                total[k:k + thick, CH * j + part * t:CH * j + part * (t + 1)]
                for k in range(0, wide, thick) for j in range(taps)
            ]
            piece = jnp.concatenate(pieces, axis=1)
            zfull[m][t] = piece
            zsend[m][t] = piece.astype(BF16)
        copies3[m] = []
        for d in range(1, spans):
            to = lax.rem(span + d, spans)
            cp = remote(zsend[m].at[to], got3[m].at[d - 1], s3.at[m, d - 1], r3.at[m, d - 1], tm=to)
            cp.start()
            copies3[m].append(cp)

    def tap_row(role):
        return {OWN: 1, CORE: 2 * parity, FAR: 2 - 2 * parity}[role]

    def finish(m):
        final = zfull[m][span]
        for d, cp in enumerate(copies3[m]):
            cp.wait()
            final = final + got3[m][d].astype(F32)
        taps = 3 * len(PARTS[m])
        n = taps * part
        final = jnp.concatenate([final[:, k * n:(k + 1) * n] for k in range(wide // thick)], axis=0) * factor
        final = final.T
        out = []
        for spot, (role, d) in enumerate(PARTS[m]):
            for c in range(3):
                j = 3 * spot + c
                share_ref[9 * (2 - d) + 3 * tap_row(role) + c] = final[part * j:part * (j + 1)]
            taps_of = pl.ds(9 * (2 - d) + 3 * tap_row(role), 3)
            cp = pltpu.make_async_copy(share_ref.at[taps_of], share_hbm.at[taps_of], s_out.at[1 + 3 * role + d])
            cp.start()
            out.append(cp)
        return out

    m_rows = groups * rows

    def adjoint(f, d, n, to):
        g = jnp.concatenate(
            [wide_g[f + e, 2 - c:2 - c + groups].reshape(m_rows, WIDE) for e in range(n) for c in range(3)], axis=1
        )
        at = pl.multiple_of(3 * WIDE * d, LANES)
        acc[to] = lax.dot_general(
            g, kern_n[:, pl.ds(at, 3 * WIDE * n)], (((1,), (1,)), ((), ())), preferred_element_type=F32
        ).reshape(groups, rows, CH)

    def near_frames(t, carry):
        adjoint(t, 0, 3, t)
        return carry

    def third_frame(i, carry):
        adjoint(2 + 2 * i, i, 2, 2 + 2 * i)
        return carry

    def fourth_frame(i, carry):
        adjoint(3 + i, 2 * i, 1, 3 + 2 * i)
        return carry

    def pack_kern(k, carry):
        for d in range(3):
            for c in range(3):
                for role in range(3):
                    at = WIDE * (3 * d + c) + CH * role
                    lines = pl.ds(pl.multiple_of(k * 16, 16), 16)
                    kern_n[lines, at:at + CH] = kern[9 * (2 - d) + 3 * tap_row(role) + c, lines, :]
                at = WIDE * (3 * d + c) + 3 * CH
                kern_n[lines, at:at + WIDE - 3 * CH] = jnp.zeros((16, WIDE - 3 * CH), BF16)
        return carry

    def write(p):
        base = tiles * p
        for s in range(slots):
            cells_of = []
            for q in range(2):
                v = acc[s, 2 * p + q] + acc[4, 2 * p + q] * where(s == count - 1)
                v = v + acc[5, 2 * p + q] * where(s == count - 2)
                cells_of.append(v * slope[s, 2 * p + q])
            v = jnp.concatenate(cells_of, axis=1)
            for t in range(tiles):
                tmp[base + t, rows * s:rows * (s + 1)] = v[:, LANES * t:LANES * (t + 1)]
        for k in range(quarters):
            at = k * groups * CH + p * PAIR
            for b in range(batch):
                for t in range(tiles):
                    v = tmp[base + t, pl.ds(batch * k + b, slots, stride=rows), :]
                    out_ref[b, :, pl.ds(at + LANES * t, LANES)] = v.astype(BF16)

    weight((OWN, CORE), 0)
    get_kern.wait()
    lax.fori_loop(0, CH // 16, pack_kern, 0)

    pl.when(jnp.logical_not(last))(tail_copies[0].wait_recv)
    tail_core[0].start()
    pl.when(has_far)(tail_far[0].start)
    for p in range(pairs):
        t_send[1, p] = (second[p].astype(F32) + t_recv[0, p].astype(F32) * where(count < 2)).astype(BF16)
    pl.when(jnp.logical_not(first))(tail_copies[1].start)
    extend(t_recv, 0, OWN)
    tail_core[0].wait_recv()
    extend(t_core, 0, CORE)
    weight((OWN, CORE), 1)
    start_core(0)

    pl.when(has_far)(far_copy.wait_recv)
    arrange(far_in, FAR)
    weight((FAR,), 0)
    start_core(1)
    start_rows(0)

    pl.when(jnp.logical_not(last))(tail_copies[1].wait_recv)
    tail_core[1].start()
    pl.when(has_far)(tail_far[1].start)
    extend(t_recv, 1, OWN)
    tail_core[1].wait_recv()
    extend(t_core, 1, CORE)
    weight((OWN, CORE), 2)
    start_core(4)
    start_rows(1)

    pl.when(has_far)(tail_far[0].wait_recv)
    extend(t_far, 0, FAR)
    weight((FAR,), 1)
    start_core(2)
    start_rows(4)

    lax.fori_loop(0, 1, near_frames, 0)
    start_spans(0)

    pl.when(has_far)(tail_far[1].wait_recv)
    extend(t_far, 1, FAR)
    weight((FAR,), 2)
    start_core(3)
    start_rows(2)
    start_spans(1)

    lax.fori_loop(1, 2, near_frames, 0)
    start_rows(3)
    start_spans(4)
    lax.fori_loop(0, 2, third_frame, 0)
    start_spans(2)
    lax.fori_loop(0, 2, fourth_frame, 0)
    start_spans(3)
    for p in range(pairs):
        write(p)
    put_out = pltpu.make_async_copy(out_ref, out_hbm, s_out.at[0])
    put_out.start()
    put_share = []
    for m in (0, 1, 4, 2, 3):
        put_share += finish(m)
    put_out.wait()
    for cp in put_share:
        cp.wait()

    core_copy.wait_send()
    pl.when(has_far)(far_copy.wait_send)
    for n in range(2):
        pl.when(jnp.logical_not(first))(tail_copies[n].wait_send)
        tail_core[n].wait_send()
        pl.when(has_far)(tail_far[n].wait_send)


def hand_over(grad_in, share_in, grad_out, share_out, grad, share, s_in, s_out):
    hops = [(grad_in.at[b], grad.at[b], grad_out.at[b]) for b in range(grad.shape[0])]
    for k in range(0, 27, 9):
        taps = pl.ds(k, 9)
        hops.append((share_in.at[taps], share.at[taps], share_out.at[taps]))
    loads = [pltpu.make_async_copy(a, b, s_in.at[n]) for n, (a, b, _) in enumerate(hops)]
    stores = [pltpu.make_async_copy(b, c, s_out.at[n]) for n, (_, b, c) in enumerate(hops)]
    for cp in loads:
        cp.start()
    for load, store in zip(loads, stores):
        load.wait()
        store.start()
    for cp in stores:
        cp.wait()


def body(inputs, cotangent, kernel, span_frames):
    batch, slots, strip, flat = inputs.shape
    cells = flat // CH
    rows = 16
    groups = cells * batch // rows
    spans, strips = lax.axis_size("tm"), lax.axis_size("rows")
    assert strip == 1 and slots == 4 and rows % batch == 0 and groups * rows == cells * batch and groups % 2 == 0
    assert strips % 2 == 0 and CH % spans == 0 and CH % strips == 0
    wide, part, half = CH // strips, CH // spans, strips // 2
    total_cells = batch * slots * spans * strip * strips * cells
    few, some = max(half - 1, 1), max(spans - 1, 1)
    thick = 16 if wide % 16 == 0 else wide
    widths = [3 * CH * len(p) for p in PARTS]
    zblocks = [(thick, wide // thick * 3 * len(p) * part) for p in PARTS]
    dma = pltpu.SemaphoreType.DMA
    parts = len(PARTS)

    def each(lead, shapes, kind):
        return tuple(pltpu.VMEM((lead,) + tuple(s), kind) for s in shapes)

    rows_of = [(wide, w) for w in widths]
    natural = (batch, slots, flat)
    paired = (groups // 2, rows, PAIR)
    tail = (2,) + paired
    anywhere = pl.BlockSpec(memory_space=pl.ANY)
    grad_in, share = pl.pallas_call(
        functools.partial(kernel_body, cells, batch, slots, strips, spans, float(total_cells) ** -0.5),
        out_shape=(
            jax.ShapeDtypeStruct(natural, BF16),
            jax.ShapeDtypeStruct((27, part, wide), F32),
        ),
        in_specs=[pl.BlockSpec(memory_space=pltpu.SMEM), anywhere, anywhere, anywhere],
        out_specs=(anywhere, anywhere),
        scratch_shapes=[
            pltpu.VMEM(natural, BF16),
            pltpu.VMEM((27, part, wide), F32),
            pltpu.VMEM(natural, BF16),
            pltpu.VMEM(natural, BF16),
            pltpu.VMEM(natural, BF16),
            pltpu.VMEM(natural, BF16),
            pltpu.VMEM((groups // 2 * (PAIR // LANES), slots * rows, LANES), F32),
            pltpu.VMEM((slots + 2, groups + 2, rows, 3 * CH), BF16),
            pltpu.VMEM((slots, groups, rows, CH), F32),
            pltpu.VMEM((slots + 2, groups + 2, rows, WIDE), BF16),
            pltpu.VMEM((slots + 2, groups, rows, CH), F32),
            pltpu.VMEM(kernel.shape, BF16),
            pltpu.VMEM((CH, 9 * WIDE), BF16),
            pltpu.VMEM(paired, BF16),
            pltpu.VMEM(tail, BF16),
            pltpu.VMEM(tail, BF16),
            pltpu.VMEM(tail, BF16),
            pltpu.VMEM(tail, BF16),
            each(strips, rows_of, F32),
            each(half, rows_of, F32),
            each(few, rows_of, BF16),
            each(few, rows_of, BF16),
            each(spans, zblocks, F32),
            each(spans, zblocks, BF16),
            each(some, zblocks, BF16),
            dma((3,)), dma((10,)), dma((2,)), dma((2,)), dma((2,)), dma((2,)), dma((2,)), dma((2,)), dma((2,)), dma((2,)),
            dma((parts, half)), dma((parts, half)), dma((parts, few)), dma((parts, few)),
            dma((parts, some)), dma((parts, some)),
        ],
        compiler_params=pltpu.CompilerParams(
            vmem_limit_bytes=56 << 20, collective_id=0, has_side_effects=True
        ),
        name="fused",
    )(span_frames, inputs.reshape(natural), cotangent.reshape(natural), kernel)
    grad_in, share = pl.pallas_call(
        hand_over,
        out_shape=(
            jax.ShapeDtypeStruct(natural, BF16),
            jax.ShapeDtypeStruct((27, part, wide), F32),
        ),
        in_specs=[anywhere, anywhere],
        out_specs=(anywhere, anywhere),
        scratch_shapes=[
            pltpu.VMEM(natural, BF16),
            pltpu.VMEM((27, part, wide), F32),
            dma((batch + 3,)), dma((batch + 3,)),
        ],
        compiler_params=pltpu.CompilerParams(vmem_limit_bytes=56 << 20),
        name="hand_over",
    )(grad_in, share)
    return grad_in.reshape(inputs.shape), share


def solution(mesh):
    return jax.shard_map(
        body,
        mesh=mesh,
        in_specs=(
            P("groups", "tm", "rows", None),
            P("groups", "tm", "rows", None),
            P(),
            P("groups"),
        ),
        out_specs=(P("groups", "tm", "rows", None), P("groups", "tm", "rows")),
        check_vma=False,
    )
```

```python
import functools

import jax
import jax.numpy as jnp
from jax import lax
from jax.experimental import pallas as pl
from jax.experimental.pallas import tpu as pltpu
from jax.sharding import PartitionSpec as P

CH = 192
PAIR = 2 * CH
LANES = 128
MESH = pl.DeviceIdType.MESH
F32, BF16 = jnp.float32, jnp.bfloat16

OWN, CORE, FAR = 0, 1, 2
WIDE = 640
CHUNKS = 4
PARTS = (((OWN, 0), (OWN, 1)), ((CORE, 0), (FAR, 0)), ((CORE, 1), (FAR, 1)), ((CORE, 2), (FAR, 2)), ((OWN, 2),))
SPANS_FIRST = (0,)
SPOT = {block: (m, n) for m, part in enumerate(PARTS) for n, block in enumerate(part)}


def down(v, n):
    return jnp.concatenate([jnp.zeros((n,) + v.shape[1:], v.dtype), v[:-n]], axis=0)


def up(v, n):
    return jnp.concatenate([v[n:], jnp.zeros((n,) + v.shape[1:], v.dtype)], axis=0)


def kernel_body(cells, batch, slots, strips, spans, factor, frames_ref, x_hbm, cot_hbm, kern_hbm, out_hbm, share_hbm,
                out_ref, share_ref, xv, cv, core_in, far_in, tmp, act, slope, wide_g, acc, kern, kern_n,
                second, t_send, t_recv, t_core, t_far, wgs, got1, send2, got2, zfull, zsend, got3, held,
                s_in, s_out, s_near, r_near, s_t, r_t, s_tc, r_tc, s_tf, r_tf, s1, r1, s2, r2, s3, r3):
    rows = 16
    quarters = rows // batch
    groups = cells // quarters
    pairs = groups // 2
    tiles = PAIR // LANES
    wide, part, half = CH // strips, CH // spans, strips // 2
    row = lax.axis_index("rows")
    span = lax.axis_index("tm")
    place = row // 2
    parity = row - 2 * place
    other = 1 - parity
    partner = 2 * place + other
    beside = row + 2 * parity - 1
    has_far = (beside >= 0) & (beside < strips)
    far_row = lax.rem(beside + strips, strips)
    first, last = span == 0, span == spans - 1
    before = lax.rem(span + spans - 1, spans)

    def strip_at(d):
        return lax.rem(place + d, half)

    def remote(src, dst, send, recv, **to):
        return pltpu.make_async_remote_copy(src, dst, send, recv, device_id=to, device_id_type=MESH)

    get_cot = pltpu.make_async_copy(cot_hbm, cv, s_in.at[0])
    get_x = pltpu.make_async_copy(x_hbm, xv, s_in.at[1])
    get_kern = pltpu.make_async_copy(kern_hbm, kern, s_in.at[2])
    get_cot.start()
    get_x.start()
    barrier = pltpu.get_barrier_semaphore()
    for d in range(1, strips):
        pl.semaphore_signal(barrier, inc=1, device_id={"rows": lax.rem(row + d, strips)}, device_id_type=MESH)
    for d in range(1, spans):
        pl.semaphore_signal(barrier, inc=1, device_id={"tm": lax.rem(span + d, spans)}, device_id_type=MESH)

    core_copy = remote(cot_hbm, core_in, s_near.at[0], r_near.at[0], rows=partner)
    far_copy = remote(cot_hbm, far_in, s_near.at[1], r_near.at[1], rows=far_row)
    cuts = [pairs * n // CHUNKS for n in range(CHUNKS + 1)]

    def tail_copy(src, dst, send, recv, **to):
        return [
            [
                remote(src.at[n, pl.ds(lo, hi - lo)], dst.at[n, pl.ds(lo, hi - lo)], send.at[n, h], recv.at[n, h], **to)
                for h, (lo, hi) in enumerate(zip(cuts, cuts[1:]))
            ]
            for n in range(2)
        ]

    tail_copies = tail_copy(t_send, t_recv, s_t, r_t, tm=before)
    tail_core = tail_copy(t_recv, t_core, s_tc, r_tc, rows=partner)
    tail_far = tail_copy(t_recv, t_far, s_tf, r_tf, rows=far_row)

    pl.semaphore_wait(barrier, strips + spans - 2)
    pl.when(has_far)(far_copy.start)
    core_copy.start()

    count = frames_ref[span]

    def where(condition):
        return jnp.where(condition, 1.0, 0.0)

    def load_pair(ref, p):
        base = tiles * p
        for k in range(quarters):
            at = k * groups * CH + p * PAIR
            for b in range(batch):
                v = ref[b, :, pl.ds(at, PAIR)].astype(F32)
                for t in range(tiles):
                    tmp[base + t, pl.ds(batch * k + b, slots, stride=rows), :] = v[:, LANES * t:LANES * (t + 1)]
        return [
            jnp.concatenate([tmp[base + t, rows * s:rows * (s + 1)] for t in range(tiles)], axis=1) for s in range(slots)
        ]

    def put(v, f, p, role):
        col = CH * role
        wide_g[f, 2 * p + 1, :, col:col + CH] = v[:, :CH]
        wide_g[f, 2 * p + 2, :, col:col + CH] = v[:, CH:]

    def edges(frames, role):
        lanes = pl.ds(CH * role, CH)
        for f in frames:
            wide_g[f, 0, :, lanes] = down(wide_g[f, groups, :, lanes], batch)
            wide_g[f, groups + 1, :, lanes] = up(wide_g[f, 1, :, lanes], batch)

    def arrange(ref, role):
        def one(p):
            for s, v in enumerate(load_pair(ref, p)):
                v = (v * where(s < count) if s else v).astype(BF16)
                put(v, s, p, role)
                if role == OWN and s == 0:
                    t_send[0, p] = v
                if role == OWN and s == 1:
                    second[p] = v

        for p in range(pairs):
            one(p)
        edges(range(slots), role)

    def extend(tails, n, role):
        for p in range(pairs):
            put(tails[n, p], slots + n, p, role)
        edges([slots + n], role)

    def blank(g, carry):
        for f in range(slots + 2):
            wide_g[f, g, :, 3 * CH:] = jnp.zeros((rows, WIDE - 3 * CH), BF16)
        return carry

    lax.fori_loop(0, groups + 2, blank, 0, unroll=4)

    @pl.when(last)
    def _():
        t_recv[...] = jnp.zeros(t_recv.shape, BF16)

    @pl.when(jnp.logical_not(has_far))
    def _():
        far_in[...] = jnp.zeros(far_in.shape, BF16)
        t_far[...] = jnp.zeros(t_far.shape, BF16)

    get_cot.wait()
    get_kern.start()
    arrange(cv, OWN)

    @pl.when(jnp.logical_not(first))
    def _():
        for cp in tail_copies[0]:
            cp.start()

    def put_act(v, f, p):
        for q in range(2):
            cell = v[:, CH * q:CH * (q + 1)]
            for c in range(3):
                act[f, 2 * p + q + 2 - c, :, CH * c:CH * (c + 1)] = cell

    def activate(p):
        at_end, ahead = [jnp.zeros((rows, PAIR), F32)] * 2
        for s, xf in enumerate(load_pair(xv, p)):
            on = where(s < count)
            sig = 1.0 / (1.0 + jnp.exp(-xf))
            a = xf * sig * on
            put_act(a.astype(BF16), s, p)
            at_end = at_end + a * where(s == count - 1)
            ahead = ahead + a * where(s == count - 2)
            v = sig * (1.0 + xf * (1.0 - sig)) * on
            for q in range(2):
                slope[s, 2 * p + q] = v[:, CH * q:CH * (q + 1)]
        put_act(ahead.astype(BF16), slots, p)
        put_act(at_end.astype(BF16), slots + 1, p)

    get_x.wait()
    for p in range(pairs):
        activate(p)
    for f in range(slots + 2):
        act[f, 1, :, :CH] = down(act[f, groups + 1, :, :CH], batch)
        act[f, groups, :, 2 * CH:] = up(act[f, 0, :, 2 * CH:], batch)

    core_copy.wait_recv()
    arrange(core_in, CORE)

    def weight(roles, d):
        lo, n = CH * roles[0], CH * len(roles)
        m_rows = slots * groups * rows
        g = wide_g[d:d + slots, 1:groups + 1, :, lo:lo + n].reshape(m_rows, n)
        a = act[:slots - d, 1:groups + 1]
        if d:
            a = jnp.concatenate([a, act[slots + 2 - d:, 1:groups + 1]], axis=0)
        res = lax.dot_general(
            g, a.reshape(m_rows, 3 * CH), (((0,), (0,)), ((), ())), preferred_element_type=F32
        )
        for k, role in enumerate(roles):
            m, spot = SPOT[role, d]
            for s in range(strips):
                lo_row = CH * k + wide * s
                wgs[m][s, :, 3 * CH * spot:3 * CH * (spot + 1)] = res[lo_row:lo_row + wide]

    order = list(range(1, half)) + [0]
    copies1, copies2, copies3 = {}, {}, {}

    def start_core(m):
        copies1[m] = []
        for d in order:
            cp = remote(wgs[m].at[2 * strip_at(d) + other], got1[m].at[d], s1.at[m, d], r1.at[m, d], rows=partner)
            cp.start()
            copies1[m].append(cp)

    def chip_sum(m, to, d):
        theirs = got1[m][d]
        if PARTS[m][0][0] == CORE:
            theirs = jnp.concatenate([theirs[:, 3 * CH:], theirs[:, :3 * CH]], axis=1)
        return wgs[m][to] + theirs

    def start_rows(m):
        copies2[m] = []
        for d, cp in zip(order, copies1[m]):
            cp.wait()
            if d:
                to = 2 * strip_at(d) + parity
                send2[m][d - 1] = chip_sum(m, to, d).astype(BF16)
                nxt = remote(send2[m].at[d - 1], got2[m].at[d - 1], s2.at[m, d - 1], r2.at[m, d - 1], rows=to)
                nxt.start()
                copies2[m].append(nxt)

    thick = 16 if wide % 16 == 0 else wide

    def by_span(total, m):
        taps = 3 * len(PARTS[m])
        for t in range(spans):
            pieces = [
                total[k:k + thick, CH * j + part * t:CH * j + part * (t + 1)]
                for k in range(0, wide, thick) for j in range(taps)
            ]
            yield t, jnp.concatenate(pieces, axis=1)

    def start_spans(m):
        if m in SPANS_FIRST:
            for d, cp in zip(order, copies1[m]):
                cp.wait()
                for t, piece in by_span(chip_sum(m, 2 * strip_at(d) + parity, d), m):
                    zfull[m][t, d] = piece
                    zsend[m][t, d] = piece.astype(BF16)
        else:
            total = chip_sum(m, row, 0)
            for d, cp in enumerate(copies2[m]):
                cp.wait()
                total = total + got2[m][d].astype(F32)
            for t, piece in by_span(total, m):
                zfull[m][t] = piece
                zsend[m][t] = piece.astype(BF16)
        copies3[m] = []
        for d in range(1, spans):
            to = lax.rem(span + d, spans)
            cp = remote(zsend[m].at[to], got3[m].at[d - 1], s3.at[m, d - 1], r3.at[m, d - 1], tm=to)
            cp.start()
            copies3[m].append(cp)

    def tap_row(role):
        return {OWN: 1, CORE: 2 * parity, FAR: 2 - 2 * parity}[role]

    def span_sum(m):
        final = zfull[m][span]
        for d, cp in enumerate(copies3[m]):
            cp.wait()
            final = final + got3[m][d].astype(F32)
        return final

    def end_rows(m):
        final = span_sum(m)
        held[...] = final[0]
        copies2[m] = []
        for d in range(1, half):
            send2[m][d - 1] = final[d].astype(BF16)
            cp = remote(send2[m].at[d - 1], got2[m].at[d - 1], s2.at[m, d - 1], r2.at[m, d - 1],
                        rows=2 * strip_at(d) + parity)
            cp.start()
            copies2[m].append(cp)

    def finish(m):
        if m in SPANS_FIRST:
            final = held[...]
            for d, cp in enumerate(copies2[m]):
                cp.wait()
                final = final + got2[m][d].astype(F32)
        else:
            final = span_sum(m)
        taps = 3 * len(PARTS[m])
        n = taps * part
        final = jnp.concatenate([final[:, k * n:(k + 1) * n] for k in range(wide // thick)], axis=0) * factor
        final = final.T
        out = []
        for spot, (role, d) in enumerate(PARTS[m]):
            for c in range(3):
                j = 3 * spot + c
                share_ref[9 * (2 - d) + 3 * tap_row(role) + c] = final[part * j:part * (j + 1)]
            taps_of = pl.ds(9 * (2 - d) + 3 * tap_row(role), 3)
            cp = pltpu.make_async_copy(share_ref.at[taps_of], share_hbm.at[taps_of], s_out.at[1 + 3 * role + d])
            cp.start()
            out.append(cp)
        return out

    m_rows = groups * rows

    def adjoint(f, d, n, to):
        g = jnp.concatenate(
            [wide_g[f + e, 2 - c:2 - c + groups].reshape(m_rows, WIDE) for e in range(n) for c in range(3)], axis=1
        )
        at = pl.multiple_of(3 * WIDE * d, LANES)
        acc[to] = lax.dot_general(
            g, kern_n[:, pl.ds(at, 3 * WIDE * n)], (((1,), (1,)), ((), ())), preferred_element_type=F32
        ).reshape(groups, rows, CH)

    def near_frames(t, carry):
        adjoint(t, 0, 3, t)
        return carry

    def third_frame(i, carry):
        adjoint(2 + 2 * i, i, 2, 2 + 2 * i)
        return carry

    def fourth_frame(i, carry):
        adjoint(3 + i, 2 * i, 1, 3 + 2 * i)
        return carry

    def pack_kern(k, carry):
        for d in range(3):
            for c in range(3):
                for role in range(3):
                    at = WIDE * (3 * d + c) + CH * role
                    lines = pl.ds(pl.multiple_of(k * 16, 16), 16)
                    kern_n[lines, at:at + CH] = kern[9 * (2 - d) + 3 * tap_row(role) + c, lines, :]
                at = WIDE * (3 * d + c) + 3 * CH
                kern_n[lines, at:at + WIDE - 3 * CH] = jnp.zeros((16, WIDE - 3 * CH), BF16)
        return carry

    def write(p):
        base = tiles * p
        for s in range(slots):
            cells_of = []
            for q in range(2):
                v = acc[s, 2 * p + q] + acc[4, 2 * p + q] * where(s == count - 1)
                v = v + acc[5, 2 * p + q] * where(s == count - 2)
                cells_of.append(v * slope[s, 2 * p + q])
            v = jnp.concatenate(cells_of, axis=1)
            for t in range(tiles):
                tmp[base + t, rows * s:rows * (s + 1)] = v[:, LANES * t:LANES * (t + 1)]
        for k in range(quarters):
            at = k * groups * CH + p * PAIR
            for b in range(batch):
                for t in range(tiles):
                    v = tmp[base + t, pl.ds(batch * k + b, slots, stride=rows), :]
                    out_ref[b, :, pl.ds(at + LANES * t, LANES)] = v.astype(BF16)

    weight((OWN, CORE), 0)
    get_kern.wait()
    lax.fori_loop(0, CH // 16, pack_kern, 0)

    def forward(n, h):
        pl.when(jnp.logical_not(last))(tail_copies[n][h].wait_recv)
        pl.when(has_far)(tail_far[n][h].start)
        tail_core[n][h].start()

    for h in range(CHUNKS):
        forward(0, h)
        for p in range(cuts[h], cuts[h + 1]):
            t_send[1, p] = (second[p].astype(F32) + t_recv[0, p].astype(F32) * where(count < 2)).astype(BF16)
        pl.when(jnp.logical_not(first))(tail_copies[1][h].start)

    def from_core(n):
        for cp in tail_core[n]:
            cp.wait_recv()
        extend(t_core, n, CORE)

    def from_far(n):
        @pl.when(has_far)
        def _():
            for cp in tail_far[n]:
                cp.wait_recv()

        extend(t_far, n, FAR)

    extend(t_recv, 0, OWN)
    from_core(0)
    weight((OWN, CORE), 1)
    start_core(0)

    for h in range(CHUNKS):
        forward(1, h)
    start_spans(0)
    extend(t_recv, 1, OWN)
    from_core(1)
    weight((OWN, CORE), 2)
    start_core(4)

    pl.when(has_far)(far_copy.wait_recv)
    arrange(far_in, FAR)
    weight((FAR,), 0)
    start_core(1)
    start_rows(4)
    from_far(0)
    weight((FAR,), 1)
    start_core(2)
    start_rows(1)

    from_far(1)
    weight((FAR,), 2)
    start_core(3)
    start_rows(2)
    lax.fori_loop(0, 1, near_frames, 0)
    start_rows(3)
    start_spans(4)
    start_spans(1)
    lax.fori_loop(1, 2, near_frames, 0)
    start_spans(2)
    lax.fori_loop(0, 2, third_frame, 0)
    start_spans(3)
    end_rows(0)
    lax.fori_loop(0, 2, fourth_frame, 0)
    for p in range(pairs):
        write(p)
    put_out = pltpu.make_async_copy(out_ref, out_hbm, s_out.at[0])
    put_out.start()
    put_share = []
    for m in (4, 1, 0, 2, 3):
        put_share += finish(m)
    put_out.wait()
    for cp in put_share:
        cp.wait()

    core_copy.wait_send()
    pl.when(has_far)(far_copy.wait_send)

    def sent(family):
        for n in range(2):
            for cp in family[n]:
                cp.wait_send()

    sent(tail_core)
    pl.when(jnp.logical_not(first))(lambda: sent(tail_copies))
    pl.when(has_far)(lambda: sent(tail_far))


def hand_over(grad_in, share_in, grad_out, share_out, grad, share, s_in, s_out):
    hops = [(grad_in.at[b], grad.at[b], grad_out.at[b]) for b in range(grad.shape[0])]
    for k in range(0, 27, 9):
        taps = pl.ds(k, 9)
        hops.append((share_in.at[taps], share.at[taps], share_out.at[taps]))
    loads = [pltpu.make_async_copy(a, b, s_in.at[n]) for n, (a, b, _) in enumerate(hops)]
    stores = [pltpu.make_async_copy(b, c, s_out.at[n]) for n, (_, b, c) in enumerate(hops)]
    for cp in loads:
        cp.start()
    for load, store in zip(loads, stores):
        load.wait()
        store.start()
    for cp in stores:
        cp.wait()


def body(inputs, cotangent, kernel, span_frames):
    batch, slots, strip, flat = inputs.shape
    cells = flat // CH
    rows = 16
    groups = cells * batch // rows
    spans, strips = lax.axis_size("tm"), lax.axis_size("rows")
    assert strip == 1 and slots == 4 and rows % batch == 0 and groups * rows == cells * batch and groups % 2 == 0
    assert strips % 2 == 0 and CH % spans == 0 and CH % strips == 0
    wide, part, half = CH // strips, CH // spans, strips // 2
    total_cells = batch * slots * spans * strip * strips * cells
    few, some = max(half - 1, 1), max(spans - 1, 1)
    thick = 16 if wide % 16 == 0 else wide
    widths = [3 * CH * len(p) for p in PARTS]
    zblocks = [(thick, wide // thick * 3 * len(p) * part) for p in PARTS]
    dma = pltpu.SemaphoreType.DMA
    parts = len(PARTS)

    def each(lead, shapes, kind):
        return tuple(pltpu.VMEM((lead,) + tuple(s), kind) for s in shapes)

    rows_of = [(wide, w) for w in widths]
    row_sends = [zblocks[m] if m in SPANS_FIRST else rows_of[m] for m in range(parts)]
    span_sends = [((half,) if m in SPANS_FIRST else ()) + zblocks[m] for m in range(parts)]
    natural = (batch, slots, flat)
    paired = (groups // 2, rows, PAIR)
    tail = (2,) + paired
    anywhere = pl.BlockSpec(memory_space=pl.ANY)
    grad_in, share = pl.pallas_call(
        functools.partial(kernel_body, cells, batch, slots, strips, spans, float(total_cells) ** -0.5),
        out_shape=(
            jax.ShapeDtypeStruct(natural, BF16),
            jax.ShapeDtypeStruct((27, part, wide), F32),
        ),
        in_specs=[pl.BlockSpec(memory_space=pltpu.SMEM), anywhere, anywhere, anywhere],
        out_specs=(anywhere, anywhere),
        scratch_shapes=[
            pltpu.VMEM(natural, BF16),
            pltpu.VMEM((27, part, wide), F32),
            pltpu.VMEM(natural, BF16),
            pltpu.VMEM(natural, BF16),
            pltpu.VMEM(natural, BF16),
            pltpu.VMEM(natural, BF16),
            pltpu.VMEM((groups // 2 * (PAIR // LANES), slots * rows, LANES), F32),
            pltpu.VMEM((slots + 2, groups + 2, rows, 3 * CH), BF16),
            pltpu.VMEM((slots, groups, rows, CH), F32),
            pltpu.VMEM((slots + 2, groups + 2, rows, WIDE), BF16),
            pltpu.VMEM((slots + 2, groups, rows, CH), F32),
            pltpu.VMEM(kernel.shape, BF16),
            pltpu.VMEM((CH, 9 * WIDE), BF16),
            pltpu.VMEM(paired, BF16),
            pltpu.VMEM(tail, BF16),
            pltpu.VMEM(tail, BF16),
            pltpu.VMEM(tail, BF16),
            pltpu.VMEM(tail, BF16),
            each(strips, rows_of, F32),
            each(half, rows_of, F32),
            each(few, row_sends, BF16),
            each(few, row_sends, BF16),
            each(spans, span_sends, F32),
            each(spans, span_sends, BF16),
            each(some, span_sends, BF16),
            pltpu.VMEM(zblocks[SPANS_FIRST[0]], F32),
            dma((3,)), dma((10,)), dma((2,)), dma((2,)),
            dma((2, CHUNKS)), dma((2, CHUNKS)), dma((2, CHUNKS)), dma((2, CHUNKS)), dma((2, CHUNKS)), dma((2, CHUNKS)),
            dma((parts, half)), dma((parts, half)), dma((parts, few)), dma((parts, few)),
            dma((parts, some)), dma((parts, some)),
        ],
        compiler_params=pltpu.CompilerParams(
            vmem_limit_bytes=56 << 20, collective_id=0, has_side_effects=True
        ),
        name="fused",
    )(span_frames, inputs.reshape(natural), cotangent.reshape(natural), kernel)
    grad_in, share = pl.pallas_call(
        hand_over,
        out_shape=(
            jax.ShapeDtypeStruct(natural, BF16),
            jax.ShapeDtypeStruct((27, part, wide), F32),
        ),
        in_specs=[anywhere, anywhere],
        out_specs=(anywhere, anywhere),
        scratch_shapes=[
            pltpu.VMEM(natural, BF16),
            pltpu.VMEM((27, part, wide), F32),
            dma((batch + 3,)), dma((batch + 3,)),
        ],
        compiler_params=pltpu.CompilerParams(vmem_limit_bytes=56 << 20),
        name="hand_over",
    )(grad_in, share)
    return grad_in.reshape(inputs.shape), share


def solution(mesh):
    return jax.shard_map(
        body,
        mesh=mesh,
        in_specs=(
            P("groups", "tm", "rows", None),
            P("groups", "tm", "rows", None),
            P(),
            P("groups"),
        ),
        out_specs=(P("groups", "tm", "rows", None), P("groups", "tm", "rows")),
        check_vma=False,
    )
```

```python
import functools

import jax
import jax.numpy as jnp
from jax import lax
from jax.experimental import pallas as pl
from jax.experimental.pallas import tpu as pltpu
from jax.sharding import PartitionSpec as P

CH = 192
PAIR = 2 * CH
LANES = 128
MESH = pl.DeviceIdType.MESH
F32, BF16 = jnp.float32, jnp.bfloat16

OWN, CORE, FAR = 0, 1, 2
WIDE = 640
CHUNKS = 2
PARTS = (((OWN, 0), (OWN, 1)), ((CORE, 0), (FAR, 0)), ((CORE, 1), (FAR, 1)), ((CORE, 2), (FAR, 2)), ((OWN, 2),))
SPANS_FIRST = (0, 4)
SPOT = {block: (m, n) for m, part in enumerate(PARTS) for n, block in enumerate(part)}


def down(v, n):
    return jnp.concatenate([jnp.zeros((n,) + v.shape[1:], v.dtype), v[:-n]], axis=0)


def up(v, n):
    return jnp.concatenate([v[n:], jnp.zeros((n,) + v.shape[1:], v.dtype)], axis=0)


def kernel_body(cells, batch, slots, strips, spans, factor, frames_ref, x_hbm, cot_hbm, kern_hbm, out_hbm, share_hbm,
                out_ref, share_ref, xv, cv, core_in, far_in, tmp, act, slope, wide_g, acc, kern, kern_n,
                second, t_send, t_recv, t_core, t_far, wgs, got1, send2, got2, zfull, zsend, got3, held,
                s_in, s_out, s_near, r_near, s_t, r_t, s_tc, r_tc, s_tf, r_tf, s1, r1, s2, r2, s3, r3):
    rows = 16
    quarters = rows // batch
    groups = cells // quarters
    pairs = groups // 2
    tiles = PAIR // LANES
    wide, part, half = CH // strips, CH // spans, strips // 2
    row = lax.axis_index("rows")
    span = lax.axis_index("tm")
    place = row // 2
    parity = row - 2 * place
    other = 1 - parity
    partner = 2 * place + other
    beside = row + 2 * parity - 1
    has_far = (beside >= 0) & (beside < strips)
    far_row = lax.rem(beside + strips, strips)
    first, last = span == 0, span == spans - 1
    before = lax.rem(span + spans - 1, spans)

    def strip_at(d):
        return lax.rem(place + d, half)

    def remote(src, dst, send, recv, **to):
        return pltpu.make_async_remote_copy(src, dst, send, recv, device_id=to, device_id_type=MESH)

    get_cot = pltpu.make_async_copy(cot_hbm, cv, s_in.at[0])
    get_x = pltpu.make_async_copy(x_hbm, xv, s_in.at[1])
    get_kern = pltpu.make_async_copy(kern_hbm, kern, s_in.at[2])
    get_cot.start()
    get_x.start()
    barrier = pltpu.get_barrier_semaphore()
    for d in range(1, strips):
        pl.semaphore_signal(barrier, inc=1, device_id={"rows": lax.rem(row + d, strips)}, device_id_type=MESH)
    for d in range(1, spans):
        pl.semaphore_signal(barrier, inc=1, device_id={"tm": lax.rem(span + d, spans)}, device_id_type=MESH)

    core_copy = remote(cot_hbm, core_in, s_near.at[0], r_near.at[0], rows=partner)
    far_copy = remote(cot_hbm, far_in, s_near.at[1], r_near.at[1], rows=far_row)
    cuts = [pairs * n // CHUNKS for n in range(CHUNKS + 1)]

    def tail_copy(src, dst, send, recv, **to):
        return [
            [
                remote(src.at[n, pl.ds(lo, hi - lo)], dst.at[n, pl.ds(lo, hi - lo)], send.at[n, h], recv.at[n, h], **to)
                for h, (lo, hi) in enumerate(zip(cuts, cuts[1:]))
            ]
            for n in range(2)
        ]

    tail_copies = tail_copy(t_send, t_recv, s_t, r_t, tm=before)
    tail_core = tail_copy(t_recv, t_core, s_tc, r_tc, rows=partner)
    tail_far = tail_copy(t_recv, t_far, s_tf, r_tf, rows=far_row)

    pl.semaphore_wait(barrier, strips + spans - 2)
    pl.when(has_far)(far_copy.start)
    core_copy.start()

    count = frames_ref[span]

    def where(condition):
        return jnp.where(condition, 1.0, 0.0)

    def load_pair(ref, p):
        base = tiles * p
        for k in range(quarters):
            at = k * groups * CH + p * PAIR
            for b in range(batch):
                v = ref[b, :, pl.ds(at, PAIR)].astype(F32)
                for t in range(tiles):
                    tmp[base + t, pl.ds(batch * k + b, slots, stride=rows), :] = v[:, LANES * t:LANES * (t + 1)]
        return [
            jnp.concatenate([tmp[base + t, rows * s:rows * (s + 1)] for t in range(tiles)], axis=1) for s in range(slots)
        ]

    def put(v, f, p, role):
        col = CH * role
        wide_g[f, 2 * p + 1, :, col:col + CH] = v[:, :CH]
        wide_g[f, 2 * p + 2, :, col:col + CH] = v[:, CH:]

    def edges(frames, role):
        lanes = pl.ds(CH * role, CH)
        for f in frames:
            wide_g[f, 0, :, lanes] = down(wide_g[f, groups, :, lanes], batch)
            wide_g[f, groups + 1, :, lanes] = up(wide_g[f, 1, :, lanes], batch)

    def arrange(ref, role):
        def one(p):
            for s, v in enumerate(load_pair(ref, p)):
                v = (v * where(s < count) if s else v).astype(BF16)
                put(v, s, p, role)
                if role == OWN and s == 0:
                    t_send[0, p] = v
                if role == OWN and s == 1:
                    second[p] = v

        for p in range(pairs):
            one(p)
        edges(range(slots), role)

    def extend(tails, n, role):
        for p in range(pairs):
            put(tails[n, p], slots + n, p, role)
        edges([slots + n], role)

    def blank(g, carry):
        for f in range(slots + 2):
            wide_g[f, g, :, 3 * CH:] = jnp.zeros((rows, WIDE - 3 * CH), BF16)
        return carry

    lax.fori_loop(0, groups + 2, blank, 0, unroll=4)

    @pl.when(last)
    def _():
        t_recv[...] = jnp.zeros(t_recv.shape, BF16)

    @pl.when(jnp.logical_not(has_far))
    def _():
        far_in[...] = jnp.zeros(far_in.shape, BF16)
        t_far[...] = jnp.zeros(t_far.shape, BF16)

    get_cot.wait()
    get_kern.start()
    arrange(cv, OWN)

    @pl.when(jnp.logical_not(first))
    def _():
        for cp in tail_copies[0]:
            cp.start()

    def put_act(v, f, p):
        for q in range(2):
            cell = v[:, CH * q:CH * (q + 1)]
            for c in range(3):
                act[f, 2 * p + q + 2 - c, :, CH * c:CH * (c + 1)] = cell

    def activate(p):
        at_end, ahead = [jnp.zeros((rows, PAIR), F32)] * 2
        for s, xf in enumerate(load_pair(xv, p)):
            on = where(s < count)
            sig = 1.0 / (1.0 + jnp.exp(-xf))
            a = xf * sig * on
            put_act(a.astype(BF16), s, p)
            at_end = at_end + a * where(s == count - 1)
            ahead = ahead + a * where(s == count - 2)
            v = sig * (1.0 + xf * (1.0 - sig)) * on
            for q in range(2):
                slope[s, 2 * p + q] = v[:, CH * q:CH * (q + 1)]
        put_act(ahead.astype(BF16), slots, p)
        put_act(at_end.astype(BF16), slots + 1, p)

    get_x.wait()
    for p in range(pairs):
        activate(p)
    for f in range(slots + 2):
        act[f, 1, :, :CH] = down(act[f, groups + 1, :, :CH], batch)
        act[f, groups, :, 2 * CH:] = up(act[f, 0, :, 2 * CH:], batch)

    core_copy.wait_recv()
    arrange(core_in, CORE)

    def weight(roles, d):
        lo, n = CH * roles[0], CH * len(roles)
        m_rows = slots * groups * rows
        g = wide_g[d:d + slots, 1:groups + 1, :, lo:lo + n].reshape(m_rows, n)
        a = act[:slots - d, 1:groups + 1]
        if d:
            a = jnp.concatenate([a, act[slots + 2 - d:, 1:groups + 1]], axis=0)
        res = lax.dot_general(
            g, a.reshape(m_rows, 3 * CH), (((0,), (0,)), ((), ())), preferred_element_type=F32
        )
        for k, role in enumerate(roles):
            m, spot = SPOT[role, d]
            for s in range(strips):
                lo_row = CH * k + wide * s
                wgs[m][s, :, 3 * CH * spot:3 * CH * (spot + 1)] = res[lo_row:lo_row + wide]

    order = list(range(1, half)) + [0]
    copies1, copies2, copies3 = {}, {}, {}

    def start_core(m):
        copies1[m] = []
        for d in order:
            cp = remote(wgs[m].at[2 * strip_at(d) + other], got1[m].at[d], s1.at[m, d], r1.at[m, d], rows=partner)
            cp.start()
            copies1[m].append(cp)

    def chip_sum(m, to, d):
        theirs = got1[m][d]
        if PARTS[m][0][0] == CORE:
            theirs = jnp.concatenate([theirs[:, 3 * CH:], theirs[:, :3 * CH]], axis=1)
        return wgs[m][to] + theirs

    def start_rows(m):
        copies2[m] = []
        for d, cp in zip(order, copies1[m]):
            cp.wait()
            if d:
                to = 2 * strip_at(d) + parity
                send2[m][d - 1] = chip_sum(m, to, d).astype(BF16)
                nxt = remote(send2[m].at[d - 1], got2[m].at[d - 1], s2.at[m, d - 1], r2.at[m, d - 1], rows=to)
                nxt.start()
                copies2[m].append(nxt)

    thick = 16 if wide % 16 == 0 else wide

    def by_span(total, m):
        taps = 3 * len(PARTS[m])
        for t in range(spans):
            pieces = [
                total[k:k + thick, CH * j + part * t:CH * j + part * (t + 1)]
                for k in range(0, wide, thick) for j in range(taps)
            ]
            yield t, jnp.concatenate(pieces, axis=1)

    def start_spans(m):
        if m in SPANS_FIRST:
            for d, cp in zip(order, copies1[m]):
                cp.wait()
                for t, piece in by_span(chip_sum(m, 2 * strip_at(d) + parity, d), m):
                    zfull[m][t, d] = piece
                    zsend[m][t, d] = piece.astype(BF16)
        else:
            total = chip_sum(m, row, 0)
            for d, cp in enumerate(copies2[m]):
                cp.wait()
                total = total + got2[m][d].astype(F32)
            for t, piece in by_span(total, m):
                zfull[m][t] = piece
                zsend[m][t] = piece.astype(BF16)
        copies3[m] = []
        for d in range(1, spans):
            to = lax.rem(span + d, spans)
            cp = remote(zsend[m].at[to], got3[m].at[d - 1], s3.at[m, d - 1], r3.at[m, d - 1], tm=to)
            cp.start()
            copies3[m].append(cp)

    def tap_row(role):
        return {OWN: 1, CORE: 2 * parity, FAR: 2 - 2 * parity}[role]

    def span_sum(m):
        final = zfull[m][span]
        for d, cp in enumerate(copies3[m]):
            cp.wait()
            final = final + got3[m][d].astype(F32)
        return final

    def end_rows(m):
        final = span_sum(m)
        held[SPANS_FIRST.index(m)][...] = final[0]
        copies2[m] = []
        for d in range(1, half):
            send2[m][d - 1] = final[d].astype(BF16)
            cp = remote(send2[m].at[d - 1], got2[m].at[d - 1], s2.at[m, d - 1], r2.at[m, d - 1],
                        rows=2 * strip_at(d) + parity)
            cp.start()
            copies2[m].append(cp)

    def finish(m):
        if m in SPANS_FIRST:
            final = held[SPANS_FIRST.index(m)][...]
            for d, cp in enumerate(copies2[m]):
                cp.wait()
                final = final + got2[m][d].astype(F32)
        else:
            final = span_sum(m)
        taps = 3 * len(PARTS[m])
        n = taps * part
        final = jnp.concatenate([final[:, k * n:(k + 1) * n] for k in range(wide // thick)], axis=0) * factor
        final = final.T
        out = []
        for spot, (role, d) in enumerate(PARTS[m]):
            for c in range(3):
                j = 3 * spot + c
                share_ref[9 * (2 - d) + 3 * tap_row(role) + c] = final[part * j:part * (j + 1)]
            taps_of = pl.ds(9 * (2 - d) + 3 * tap_row(role), 3)
            cp = pltpu.make_async_copy(share_ref.at[taps_of], share_hbm.at[taps_of], s_out.at[1 + 3 * role + d])
            cp.start()
            out.append(cp)
        return out

    m_rows = groups * rows

    def adjoint(f, d, n, to):
        g = jnp.concatenate(
            [wide_g[f + e, 2 - c:2 - c + groups].reshape(m_rows, WIDE) for e in range(n) for c in range(3)], axis=1
        )
        at = pl.multiple_of(3 * WIDE * d, LANES)
        acc[to] = lax.dot_general(
            g, kern_n[:, pl.ds(at, 3 * WIDE * n)], (((1,), (1,)), ((), ())), preferred_element_type=F32
        ).reshape(groups, rows, CH)

    def near_frames(t, carry):
        adjoint(t, 0, 3, t)
        return carry

    def third_frame(i, carry):
        adjoint(2 + 2 * i, i, 2, 2 + 2 * i)
        return carry

    def fourth_frame(i, carry):
        adjoint(3 + i, 2 * i, 1, 3 + 2 * i)
        return carry

    def pack_kern(k, carry):
        for d in range(3):
            for c in range(3):
                for role in range(3):
                    at = WIDE * (3 * d + c) + CH * role
                    lines = pl.ds(pl.multiple_of(k * 16, 16), 16)
                    kern_n[lines, at:at + CH] = kern[9 * (2 - d) + 3 * tap_row(role) + c, lines, :]
                at = WIDE * (3 * d + c) + 3 * CH
                kern_n[lines, at:at + WIDE - 3 * CH] = jnp.zeros((16, WIDE - 3 * CH), BF16)
        return carry

    def write(p):
        base = tiles * p
        for s in range(slots):
            cells_of = []
            for q in range(2):
                v = acc[s, 2 * p + q] + acc[4, 2 * p + q] * where(s == count - 1)
                v = v + acc[5, 2 * p + q] * where(s == count - 2)
                cells_of.append(v * slope[s, 2 * p + q])
            v = jnp.concatenate(cells_of, axis=1)
            for t in range(tiles):
                tmp[base + t, rows * s:rows * (s + 1)] = v[:, LANES * t:LANES * (t + 1)]
        for k in range(quarters):
            at = k * groups * CH + p * PAIR
            for b in range(batch):
                for t in range(tiles):
                    v = tmp[base + t, pl.ds(batch * k + b, slots, stride=rows), :]
                    out_ref[b, :, pl.ds(at + LANES * t, LANES)] = v.astype(BF16)

    weight((OWN, CORE), 0)
    get_kern.wait()
    lax.fori_loop(0, CH // 16, pack_kern, 0)

    def forward(n, h):
        pl.when(jnp.logical_not(last))(tail_copies[n][h].wait_recv)
        pl.when(has_far)(tail_far[n][h].start)
        tail_core[n][h].start()

    for h in range(CHUNKS):
        forward(0, h)
        for p in range(cuts[h], cuts[h + 1]):
            t_send[1, p] = (second[p].astype(F32) + t_recv[0, p].astype(F32) * where(count < 2)).astype(BF16)
        pl.when(jnp.logical_not(first))(tail_copies[1][h].start)

    def from_core(n):
        for cp in tail_core[n]:
            cp.wait_recv()
        extend(t_core, n, CORE)

    def from_far(n):
        @pl.when(has_far)
        def _():
            for cp in tail_far[n]:
                cp.wait_recv()

        extend(t_far, n, FAR)

    extend(t_recv, 0, OWN)
    from_core(0)
    weight((OWN, CORE), 1)
    start_core(0)

    for h in range(CHUNKS):
        forward(1, h)
    start_spans(0)
    extend(t_recv, 1, OWN)
    from_core(1)
    weight((OWN, CORE), 2)
    start_core(4)

    pl.when(has_far)(far_copy.wait_recv)
    arrange(far_in, FAR)
    weight((FAR,), 0)
    start_core(1)
    start_spans(4)
    from_far(0)
    weight((FAR,), 1)
    start_core(2)
    start_rows(1)

    from_far(1)
    weight((FAR,), 2)
    start_core(3)
    start_rows(2)
    lax.fori_loop(0, 1, near_frames, 0)
    start_rows(3)
    start_spans(1)
    lax.fori_loop(1, 2, near_frames, 0)
    start_spans(2)
    lax.fori_loop(0, 2, third_frame, 0)
    start_spans(3)
    end_rows(0)
    end_rows(4)
    lax.fori_loop(0, 2, fourth_frame, 0)
    for p in range(pairs):
        write(p)
    put_out = pltpu.make_async_copy(out_ref, out_hbm, s_out.at[0])
    put_out.start()
    put_share = []
    for m in (1, 0, 4, 2, 3):
        put_share += finish(m)
    put_out.wait()
    for cp in put_share:
        cp.wait()

    core_copy.wait_send()
    pl.when(has_far)(far_copy.wait_send)

    def sent(family):
        for n in range(2):
            for cp in family[n]:
                cp.wait_send()

    sent(tail_core)
    pl.when(jnp.logical_not(first))(lambda: sent(tail_copies))
    pl.when(has_far)(lambda: sent(tail_far))


def hand_over(grad_in, share_in, grad_out, share_out, grad, share, s_in, s_out):
    hops = [(grad_in.at[b], grad.at[b], grad_out.at[b]) for b in range(grad.shape[0])]
    for k in range(0, 27, 9):
        taps = pl.ds(k, 9)
        hops.append((share_in.at[taps], share.at[taps], share_out.at[taps]))
    loads = [pltpu.make_async_copy(a, b, s_in.at[n]) for n, (a, b, _) in enumerate(hops)]
    stores = [pltpu.make_async_copy(b, c, s_out.at[n]) for n, (_, b, c) in enumerate(hops)]
    for cp in loads:
        cp.start()
    for load, store in zip(loads, stores):
        load.wait()
        store.start()
    for cp in stores:
        cp.wait()


def body(inputs, cotangent, kernel, span_frames):
    batch, slots, strip, flat = inputs.shape
    cells = flat // CH
    rows = 16
    groups = cells * batch // rows
    spans, strips = lax.axis_size("tm"), lax.axis_size("rows")
    assert strip == 1 and slots == 4 and rows % batch == 0 and groups * rows == cells * batch and groups % 2 == 0
    assert strips % 2 == 0 and CH % spans == 0 and CH % strips == 0
    wide, part, half = CH // strips, CH // spans, strips // 2
    total_cells = batch * slots * spans * strip * strips * cells
    few, some = max(half - 1, 1), max(spans - 1, 1)
    thick = 16 if wide % 16 == 0 else wide
    widths = [3 * CH * len(p) for p in PARTS]
    zblocks = [(thick, wide // thick * 3 * len(p) * part) for p in PARTS]
    dma = pltpu.SemaphoreType.DMA
    parts = len(PARTS)

    def each(lead, shapes, kind):
        return tuple(pltpu.VMEM((lead,) + tuple(s), kind) for s in shapes)

    rows_of = [(wide, w) for w in widths]
    row_sends = [zblocks[m] if m in SPANS_FIRST else rows_of[m] for m in range(parts)]
    span_sends = [((half,) if m in SPANS_FIRST else ()) + zblocks[m] for m in range(parts)]
    natural = (batch, slots, flat)
    paired = (groups // 2, rows, PAIR)
    tail = (2,) + paired
    anywhere = pl.BlockSpec(memory_space=pl.ANY)
    grad_in, share = pl.pallas_call(
        functools.partial(kernel_body, cells, batch, slots, strips, spans, float(total_cells) ** -0.5),
        out_shape=(
            jax.ShapeDtypeStruct(natural, BF16),
            jax.ShapeDtypeStruct((27, part, wide), F32),
        ),
        in_specs=[pl.BlockSpec(memory_space=pltpu.SMEM), anywhere, anywhere, anywhere],
        out_specs=(anywhere, anywhere),
        scratch_shapes=[
            pltpu.VMEM(natural, BF16),
            pltpu.VMEM((27, part, wide), F32),
            pltpu.VMEM(natural, BF16),
            pltpu.VMEM(natural, BF16),
            pltpu.VMEM(natural, BF16),
            pltpu.VMEM(natural, BF16),
            pltpu.VMEM((groups // 2 * (PAIR // LANES), slots * rows, LANES), F32),
            pltpu.VMEM((slots + 2, groups + 2, rows, 3 * CH), BF16),
            pltpu.VMEM((slots, groups, rows, CH), F32),
            pltpu.VMEM((slots + 2, groups + 2, rows, WIDE), BF16),
            pltpu.VMEM((slots + 2, groups, rows, CH), F32),
            pltpu.VMEM(kernel.shape, BF16),
            pltpu.VMEM((CH, 9 * WIDE), BF16),
            pltpu.VMEM(paired, BF16),
            pltpu.VMEM(tail, BF16),
            pltpu.VMEM(tail, BF16),
            pltpu.VMEM(tail, BF16),
            pltpu.VMEM(tail, BF16),
            each(strips, rows_of, F32),
            each(half, rows_of, F32),
            each(few, row_sends, BF16),
            each(few, row_sends, BF16),
            each(spans, span_sends, F32),
            each(spans, span_sends, BF16),
            each(some, span_sends, BF16),
            tuple(pltpu.VMEM(zblocks[m], F32) for m in SPANS_FIRST),
            dma((3,)), dma((10,)), dma((2,)), dma((2,)),
            dma((2, CHUNKS)), dma((2, CHUNKS)), dma((2, CHUNKS)), dma((2, CHUNKS)), dma((2, CHUNKS)), dma((2, CHUNKS)),
            dma((parts, half)), dma((parts, half)), dma((parts, few)), dma((parts, few)),
            dma((parts, some)), dma((parts, some)),
        ],
        compiler_params=pltpu.CompilerParams(
            vmem_limit_bytes=56 << 20, collective_id=0, has_side_effects=True
        ),
        name="fused",
    )(span_frames, inputs.reshape(natural), cotangent.reshape(natural), kernel)
    grad_in, share = pl.pallas_call(
        hand_over,
        out_shape=(
            jax.ShapeDtypeStruct(natural, BF16),
            jax.ShapeDtypeStruct((27, part, wide), F32),
        ),
        in_specs=[anywhere, anywhere],
        out_specs=(anywhere, anywhere),
        scratch_shapes=[
            pltpu.VMEM(natural, BF16),
            pltpu.VMEM((27, part, wide), F32),
            dma((batch + 3,)), dma((batch + 3,)),
        ],
        compiler_params=pltpu.CompilerParams(vmem_limit_bytes=56 << 20),
        name="hand_over",
    )(grad_in, share)
    return grad_in.reshape(inputs.shape), share


def solution(mesh):
    return jax.shard_map(
        body,
        mesh=mesh,
        in_specs=(
            P("groups", "tm", "rows", None),
            P("groups", "tm", "rows", None),
            P(),
            P("groups"),
        ),
        out_specs=(P("groups", "tm", "rows", None), P("groups", "tm", "rows")),
        check_vma=False,
    )
```
